512 devices in a mesh: temp: 32 (over y, x), bond: 16 (over z, core).
Axes of the slice: x: 4, y: 8, z: 8, core: 2. Of those that a mesh axis runs over, the one named last changes fastest.
Arguments:
- tensor: float32 [2048, 4096], P(('temp', 'bond')), parts along dimension 0, may hold values from -6 to 6
- isometries: float32 [96, 64, 4096], P('temp', 'bond'), parts along dimension 0, may hold values from -0.09375 to 0.09375
Outputs:
- final_tensor: float32 [2048, 4096], P(('temp', 'bond')), parts along dimension 0
- log_density: float32 [32], P('temp'), parts along dimension 0
The draws below stay inside these ranges and needn't reach their ends.
There are 32 independent parts, one for each index of `temp`. The reference program is written for one: setup_inputs(seed, part) draws one part's arguments, and reference() takes and returns one part's arrays. A program takes and returns all parts, laid end to end along the dimension named above; each array names one. Nothing has to cross between parts.
All inputs are finite; a program needn't handle non-finite values. Where the reference program divides by a largest or mean magnitude, that divisor is 1e-20 or more.
Results may differ from the reference program's by a relative error of at most 0.00027.
Values sent between devices are 32-bit elements; how exact they have to be, the bound alone decides.
A program may use at most 64 MiB of HBM per device.

```python
import jax
import jax.numpy as jnp
from jax import lax

CHI = 64
LEVELS = 3


def shard_levels(rng, shape, cuts, low, high):
    factor_of, own = 1.0, jax.random.fold_in(rng, 6)
    for position, shards_of in cuts:
        steps = jnp.exp(jax.random.uniform(jax.random.fold_in(own, position), (shards_of,), jnp.float32, low / len(cuts), high / len(cuts)))
        factor_of = factor_of * jnp.repeat(steps, shape[position] // shards_of).reshape([-1 if axis == position else 1 for axis in range(len(shape))])
    return factor_of


def gaussian(key, extent, spread, reach, split=(), held_as=jnp.bfloat16):
    result = jax.random.normal(key, extent, jnp.float32) * spread
    if len(split) > 0:
        result = shard_levels(key, extent, split, -0.22, 0.18) * result
    return jnp.clip(result, min=-reach, max=reach).astype(held_as)


def setup_inputs(seed: int = 0, part: int = 0) -> dict:
    streams_of = jax.random.split(jax.random.key(seed), 3)
    part_keys = jax.random.split(jax.random.fold_in(streams_of[2], part), 3)
    tensor = gaussian(part_keys[0], (CHI, CHI * CHI), 1.0, 6.0, ((0, 16),), jnp.float32)
    isometries = gaussian(part_keys[1], (LEVELS, CHI, CHI * CHI), (CHI * CHI) ** -0.5, 0.09375, ((1, 16),), jnp.float32)
    return {"tensor": tensor, "isometries": isometries}


PRECISE = lax.Precision.HIGHEST
EPSILON = 1e-6


def unpack(flat):
    return flat.reshape(CHI, CHI, CHI).transpose(1, 2, 0)


def reference(tensor, isometries):
    log_density = jnp.zeros((1,), jnp.float32)
    current_flat = tensor
    for section_idx in range(LEVELS):
        current = unpack(current_flat)
        isometry = isometries[section_idx].reshape(CHI, CHI, CHI)
        inner_sum = jnp.einsum('bct,nst->nbcs', current, isometry, precision=PRECISE)
        summed = jnp.einsum('abs,nbcs->nac', current, inner_sum, precision=PRECISE)
        largest = jnp.max(jnp.abs(summed)) + EPSILON
        current_flat = summed.reshape(CHI, CHI * CHI) / largest
        log_density = log_density + jnp.log(largest) * (0.5 ** (section_idx + 1))
    return current_flat, log_density
```

```python
import functools

import jax
import jax.numpy as jnp
from jax import lax
from jax.experimental import pallas as pl
from jax.experimental.pallas import tpu as pltpu
from jax.sharding import PartitionSpec as P

EPSILON = 1e-06
PIECES = 2
UNROLL = 8
F32 = jnp.float32
BF16 = jnp.bfloat16


def split(x):
    high = x.astype(BF16)
    return high, (x - high.astype(F32)).astype(BF16)


def interleave(x, y, low):
    kept = jnp.where(low, x, y)
    moved = pltpu.roll(jnp.where(low, y, x), 64, 1)
    return jnp.where(low, kept, moved), jnp.where(low, moved, kept)


def kernel(
    levels, parts, tensor_ref, iso_ref, out_ref, log_ref,
    gathered, peaks, own_peak, spread, rows, weights, flipped, left_op, inner_hi, inner_lo, turned,
    ring_send, ring_recv, pair_send, pair_recv, peak_send, peak_recv,
):
    me = lax.axis_index("bond")
    core = lax.rem(me, 2)
    chip = me // 2
    chips = parts // 2
    far = chips // 2
    rows_own, width2 = tensor_ref.shape
    half = width2 // 2
    wide = half // PIECES

    def slot_of(offset, core):
        return lax.rem(chip + offset + chips, chips) * 2 + core

    pair = chip * 2 + (1 - core)
    signs = (1 - 2 * (chip < 2).astype(jnp.int32), 2 * (chip < 2).astype(jnp.int32) - 1)

    peers = [slot_of(offset, core) for offset in (1, -1, 2, -2)] + [pair]
    barrier = pltpu.get_barrier_semaphore()
    for peer in peers:
        pl.semaphore_signal(barrier, inc=1, device_id={"bond": peer}, device_id_type=pl.DeviceIdType.MESH)
    pl.semaphore_wait(barrier, len(peers))

    def lanes_of(q):
        return pl.ds(q * wide if isinstance(q, int) else pl.multiple_of(q * wide, 128), wide)

    def remote(ref, send_sem, recv_sem, device):
        return pltpu.make_async_remote_copy(
            src_ref=ref,
            dst_ref=ref,
            send_sem=send_sem,
            recv_sem=recv_sem,
            device_id={"bond": device},
            device_id_type=pl.DeviceIdType.MESH,
        )

    def way_of(sign):
        return (1 - sign) // 2

    def ring_copy(level, sign, total, hops, i, offset):
        q = i + way_of(sign) * (PIECES // 2) if total == far else i
        ref = gathered.at[level, slot_of(offset, core), :, lanes_of(q)]
        way = way_of(sign)
        return remote(ref, ring_send.at[level, total - 1, way, i], ring_recv.at[level, total - 1, way, i], slot_of(sign * hops, core))

    def sending(level, sign, total, i):
        hops = total if total <= 2 else total - 2
        return ring_copy(level, sign, total, hops, i, sign * (hops - total))

    def arriving(level, sign, total, i):
        return ring_copy(level, sign, total, total if total <= 2 else total - 2, i, -sign * total)

    def count(total):
        return PIECES // 2 if total == far else PIECES

    def pair_copy(level, sign, total, i, sent):
        slot = slot_of(-sign * total, core if sent else 1 - core)
        q = i + way_of(sign) * (PIECES // 2) if total == far else i
        ref = gathered.at[level, slot, :, lanes_of(q)]
        way = 0 if total == 0 else way_of(sign)
        return remote(ref, pair_send.at[level, total, way, i], pair_recv.at[level, total, way, i], pair)

    def pair_block(level, sent):
        ref = gathered.at[level, me if sent else pair]
        return remote(ref, pair_send.at[level, 0, 0, 0], pair_recv.at[level, 0, 0, 0], pair)

    def start_gather(level):
        for total in (2, 1):
            for i in range(PIECES):
                for sign in (1, -1):
                    sending(level, sign, total, i).start()
        pair_block(level, True).start()

    def receive(level, sign, total):
        for i in range(count(total)):
            arriving(level, sign, total, i).wait_recv()
            pair_copy(level, sign, total, i, True).start()

    def pair_receive(level, total):
        for sign in (1, -1):
            for i in range(count(total)):
                pair_copy(level, sign, total, i, False).wait_recv()

    def near_gather(level):
        for sign in signs:
            for i in range(PIECES):
                arriving(level, sign, 2, i).wait_recv()
                sending(level, sign, 3, i).start()
                pair_copy(level, sign, 2, i, True).start()
            for i in range(count(far)):
                sending(level, sign, far, i).start()
        for sign in signs:
            receive(level, sign, 1)
        pair_block(level, False).wait_recv()
        pair_receive(level, 1)
        pair_receive(level, 2)

    def far_gather(level):
        for total in (3, far):
            for sign in signs:
                receive(level, sign, total)
        pair_receive(level, 3)
        pair_receive(level, far)

    def wait_sent(level):
        for total in range(1, far + 1):
            for sign in (1, -1):
                for i in range(count(total)):
                    sending(level, sign, total, i).wait_send()
                    pair_copy(level, sign, total, i, True).wait_send()
        pair_block(level, True).wait_send()

    def load_isometry(level):
        pairs = iso_ref.shape[2] // 128
        for n in range(rows_own):
            for j in range(pairs):
                spread[n * pairs + j : n * pairs + j + 1, :] = iso_ref[level, n : n + 1, j * 128 : (j + 1) * 128]
        for n in range(rows_own):
            both = spread[n * pairs : (n + 1) * pairs, :]
            rows[pl.ds(n * 2 * pairs, pairs, stride=2), :] = both
            rows[pl.ds(n * 2 * pairs + 1, pairs, stride=2), :] = pltpu.roll(both, 64, 1)
        hi, lo = split(rows[...][:, :64])
        left_op[:, :64] = hi
        left_op[:, 64:128] = hi
        left_op[:, 128:192] = lo

    low_lanes = lax.broadcasted_iota(jnp.int32, (64, 128), 1) < 64
    low_rows = lax.broadcasted_iota(jnp.int32, (8, 128), 0) < 4

    def contract(level, inverse):
        left_now = left_op[...]

        def first(i, _):
            lanes = pl.ds(pl.multiple_of(i * 128, 128), 128)
            top, bottom = [], []
            for d in range(0, parts, 2):
                x, y = gathered[level, d, :, lanes], gathered[level, d + 1, :, lanes]
                top.append(jnp.where(low_rows, x, pltpu.roll(y, 4, 0)))
                bottom.append(jnp.where(low_rows, pltpu.roll(x, 4, 0), y))
            both = jnp.concatenate(top + bottom, axis=0)
            if inverse is not None:
                both = both * inverse
            flipped[pl.ds(pl.multiple_of(i * 128, 128), 128), :] = both.T
            hi, lo = split(both)
            operand = jnp.concatenate(
                [jnp.concatenate([hi[h * 64 : h * 64 + 64], lo[h * 64 : h * 64 + 64], hi[h * 64 : h * 64 + 64]], axis=0) for h in (0, 1)],
                axis=1,
            )
            inner = jnp.dot(left_now, operand, preferred_element_type=F32)
            for h in (0, 1):
                for n in range(0, rows_own, 2):
                    x = inner[n * 64 : n * 64 + 64, h * 128 : h * 128 + 128]
                    y = inner[n * 64 + 64 : n * 64 + 128, h * 128 : h * 128 + 128]
                    for b, block in enumerate(interleave(x, y, low_lanes)):
                        place = pl.ds(pl.multiple_of(h * 2048 + i * 128, 128) + b * 64, 64)
                        hi, lo = split(block)
                        inner_hi[place, n * 64 : n * 64 + 128] = hi
                        inner_lo[place, n * 64 : n * 64 + 128] = lo
            return 0

        lax.fori_loop(0, half // 128, first, 0, unroll=UNROLL)

        low32 = low_lanes[:32]
        for j in range(32):
            x = flipped[pl.ds(2 * j, 32, stride=64), :]
            y = flipped[pl.ds(2 * j + 1, 32, stride=64), :]
            block = jnp.concatenate(interleave(x, y, low32), axis=0)
            hi, lo = split(block)
            weights[:64, j * 128 : j * 128 + 128] = hi
            weights[64:, j * 128 : j * 128 + 128] = lo

        main = jnp.dot(weights[...], inner_hi[...], preferred_element_type=F32)
        rest = jnp.dot(weights[:64, :], inner_lo[...], preferred_element_type=F32)
        return main[:64] + (main[64:] + rest)

    def own_layout(summed):
        rows[:64, :] = summed[:, :128]
        rows[64:128, :] = summed[:, 128:]
        for g in (0, 1):
            x = rows[pl.ds(g * 64, 32, stride=2), :]
            y = rows[pl.ds(g * 64 + 1, 32, stride=2), :]
            for b, block in enumerate(interleave(x, y, low_lanes[:32])):
                n = 2 * g + b
                turned[n * 16 : n * 16 + 16, :] = block[:16]
                turned[64 + n * 16 : 64 + n * 16 + 16, :] = block[16:]
        return [turned[pl.ds(j, 8, stride=16), :] for j in range(16)]

    def peak_over(level, offsets, peak):
        peaks = [peak] * 4
        for offset in offsets:
            for c in (0, 1):
                block = jnp.abs(gathered[level, slot_of(offset, c)])
                for j in range(half // 128):
                    peaks[j % 4] = jnp.maximum(peaks[j % 4], block[:, j * 128 : j * 128 + 128])
        return jnp.maximum(jnp.maximum(peaks[0], peaks[1]), jnp.maximum(peaks[2], peaks[3]))

    gathered[0, me] = jnp.concatenate([tensor_ref[:, :half], tensor_ref[:, half:]], axis=0)
    start_gather(0)
    log_density = jnp.zeros((1, 1), F32)
    for level in range(levels):
        load_isometry(level)
        near_gather(level)
        peak = jnp.zeros((8, 128), F32)
        if level > 0:
            peak = peak_over(level, range(-2, 3), peak)
        far_gather(level)
        inverse = None
        if level > 0:
            peak = peak_over(level, range(3, 6), peak)
            largest = jnp.max(jnp.max(peak, axis=0, keepdims=True), axis=1, keepdims=True) + EPSILON
            log_density = log_density + jnp.log(largest) * 0.5**level
            inverse = 1.0 / largest
        tiles = own_layout(contract(level, inverse))
        if level + 1 < levels:
            for j, tile in enumerate(tiles):
                gathered[level + 1, me, :, j * 128 : j * 128 + 128] = tile
            start_gather(level + 1)

    peak = functools.reduce(jnp.maximum, [jnp.abs(tile) for tile in tiles])
    own_peak[...] = peak
    peaks[me] = peak

    def peak_copy(d):
        return pltpu.make_async_remote_copy(
            src_ref=own_peak,
            dst_ref=peaks.at[me],
            send_sem=peak_send.at[d],
            recv_sem=peak_recv.at[d],
            device_id={"bond": lax.rem(me + d, parts)},
            device_id_type=pl.DeviceIdType.MESH,
        )

    def peak_arrival(d):
        return pltpu.make_async_remote_copy(
            src_ref=own_peak,
            dst_ref=peaks.at[lax.rem(me + parts - d, parts)],
            send_sem=peak_send.at[d],
            recv_sem=peak_recv.at[d],
            device_id={"bond": lax.rem(me + d, parts)},
            device_id_type=pl.DeviceIdType.MESH,
        )

    for d in range(1, parts):
        peak_copy(d).start()
    for level in range(levels):
        wait_sent(level)
    for d in range(1, parts):
        peak_arrival(d).wait_recv()
    peak = functools.reduce(jnp.maximum, [peaks[d] for d in range(parts)])
    largest = jnp.max(jnp.max(peak, axis=0, keepdims=True), axis=1, keepdims=True) + EPSILON
    log_density = log_density + jnp.log(largest) * 0.5**levels
    inverse = 1.0 / largest
    for j, tile in enumerate(tiles):
        tile = tile * inverse
        out_ref[:, j * 128 : j * 128 + 128] = tile[:4]
        out_ref[:, half + j * 128 : half + j * 128 + 128] = tile[4:]
    log_ref[...] = jnp.broadcast_to(log_density, log_ref.shape)
    for d in range(1, parts):
        peak_copy(d).wait_send()


def solution(mesh):
    parts = mesh.shape["bond"]

    def on_device(tensor, isometries):
        levels = isometries.shape[0]
        rows, width2 = tensor.shape
        width = rows * parts
        far = parts // 4
        dma = pltpu.SemaphoreType.DMA
        vmem = pl.BlockSpec(memory_space=pltpu.VMEM)
        out, log_density = pl.pallas_call(
            functools.partial(kernel, levels, parts),
            out_shape=(jax.ShapeDtypeStruct(tensor.shape, F32), jax.ShapeDtypeStruct((1, 128), F32)),
            in_specs=[vmem, vmem],
            out_specs=(vmem, vmem),
            scratch_shapes=[
                pltpu.VMEM((levels, parts, 2 * rows, width2 // 2), F32),
                pltpu.VMEM((parts, 8, 128), F32),
                pltpu.VMEM((8, 128), F32),
                pltpu.VMEM((rows * width // 2, 128), F32),
                pltpu.VMEM((rows * width, 128), F32),
                pltpu.VMEM((2 * width, width2), BF16),
                pltpu.VMEM((width2 // 2, 128), F32),
                pltpu.VMEM((rows * width, 3 * width), BF16),
                pltpu.VMEM((width2, rows * width), BF16),
                pltpu.VMEM((width2, rows * width), BF16),
                pltpu.VMEM((128, 128), F32),
                dma((levels, far, 2, PIECES)),
                dma((levels, far, 2, PIECES)),
                dma((levels, far + 1, 2, PIECES)),
                dma((levels, far + 1, 2, PIECES)),
                dma((parts,)),
                dma((parts,)),
            ],
            compiler_params=pltpu.CompilerParams(collective_id=0, has_side_effects=True),
        )(tensor, isometries)
        return out, log_density[0, :1]

    in_specs = (P(("temp", "bond"), None), P("temp", "bond", None))
    out_specs = (P(("temp", "bond"), None), P("temp"))
    return jax.shard_map(on_device, mesh=mesh, in_specs=in_specs, out_specs=out_specs, check_vma=False)
```

```python
import functools

import jax
import jax.numpy as jnp
from jax import lax
from jax.experimental import pallas as pl
from jax.experimental.pallas import tpu as pltpu
from jax.sharding import PartitionSpec as P

EPSILON = 1e-06
PIECES = 2
UNROLL = 8
F32 = jnp.float32
BF16 = jnp.bfloat16


def split(x):
    high = x.astype(BF16)
    return high, (x - high.astype(F32)).astype(BF16)


def interleave(x, y, low):
    kept = jnp.where(low, x, y)
    moved = pltpu.roll(jnp.where(low, y, x), 64, 1)
    return jnp.where(low, kept, moved), jnp.where(low, moved, kept)


def kernel(
    levels, parts, tensor_hbm, iso_hbm, out_ref, log_ref,
    tensor_ref, iso_ref, gathered, peaks, own_peak, spread, rows, weights, flipped, left_op, inner_hi, inner_lo, turned,
    ring_send, ring_recv, pair_send, pair_recv, peak_send, peak_recv, in_sem,
):
    tensor_in = pltpu.make_async_copy(tensor_hbm, tensor_ref, in_sem.at[0])
    iso_in = pltpu.make_async_copy(iso_hbm, iso_ref, in_sem.at[1])
    tensor_in.start()
    iso_in.start()
    me = lax.axis_index("bond")
    core = lax.rem(me, 2)
    chip = me // 2
    chips = parts // 2
    far = chips // 2
    rows_own, width2 = tensor_ref.shape
    half = width2 // 2
    wide = half // PIECES

    def slot_of(offset, core):
        return lax.rem(chip + offset + chips, chips) * 2 + core

    pair = chip * 2 + (1 - core)
    signs = (1 - 2 * (chip < 2).astype(jnp.int32), 2 * (chip < 2).astype(jnp.int32) - 1)

    peers = [slot_of(offset, core) for offset in (1, -1, 2, -2)] + [pair]
    barrier = pltpu.get_barrier_semaphore()
    for peer in peers:
        pl.semaphore_signal(barrier, inc=1, device_id={"bond": peer}, device_id_type=pl.DeviceIdType.MESH)

    def lanes_of(sign, i):
        q = lax.rem(i + way_of(sign) * (PIECES // 2), PIECES)
        return pl.ds(q * wide if isinstance(q, int) else pl.multiple_of(q * wide, 128), wide)

    def remote(ref, send_sem, recv_sem, device):
        return pltpu.make_async_remote_copy(
            src_ref=ref,
            dst_ref=ref,
            send_sem=send_sem,
            recv_sem=recv_sem,
            device_id={"bond": device},
            device_id_type=pl.DeviceIdType.MESH,
        )

    def way_of(sign):
        return (1 - sign) // 2

    def ring_copy(level, sign, total, hops, i, offset):
        ref = gathered.at[level, slot_of(offset, core)]
        if total in (2, far):
            ref = ref.at[:, lanes_of(sign, i)]
        way = way_of(sign)
        return remote(ref, ring_send.at[level, total - 1, way, i], ring_recv.at[level, total - 1, way, i], slot_of(sign * hops, core))

    def sending(level, sign, total, i):
        hops = total if total <= 2 else total - 2
        return ring_copy(level, sign, total, hops, i, sign * (hops - total))

    def arriving(level, sign, total, i):
        return ring_copy(level, sign, total, total if total <= 2 else total - 2, i, -sign * total)

    def count(total):
        return PIECES // 2 if total == far else PIECES if total == 2 else 1

    def pair_copy(level, sign, total, i, sent):
        slot = slot_of(-sign * total, core if sent else 1 - core)
        ref = gathered.at[level, slot]
        if total == far:
            ref = ref.at[:, lanes_of(sign, i)]
        way = 0 if total == 0 else way_of(sign)
        return remote(ref, pair_send.at[level, total, way, i], pair_recv.at[level, total, way, i], pair)

    def pair_block(level, sent):
        ref = gathered.at[level, me if sent else pair]
        return remote(ref, pair_send.at[level, 0, 0, 0], pair_recv.at[level, 0, 0, 0], pair)

    def start_gather(level):
        for total in (2, 1):
            for i in range(count(total)):
                for sign in (1, -1):
                    sending(level, sign, total, i).start()
        pair_block(level, True).start()

    def receive(level, sign, total):
        for i in range(count(total)):
            arriving(level, sign, total, i).wait_recv()
            pair_copy(level, sign, total, i, True).start()

    def pair_receive(level, total):
        for sign in (1, -1):
            for i in range(count(total) if total == far else 1):
                pair_copy(level, sign, total, i, False).wait_recv()

    def near_gather(level):
        for sign in signs:
            for i in range(PIECES):
                arriving(level, sign, 2, i).wait_recv()
                if i < count(far):
                    sending(level, sign, far, i).start()
            sending(level, sign, 3, 0).start()
            pair_copy(level, sign, 2, 0, True).start()
        for sign in signs:
            receive(level, sign, 1)
        pair_block(level, False).wait_recv()
        pair_receive(level, 1)
        pair_receive(level, 2)

    def far_gather(level):
        for total in (far, 3):
            for sign in signs:
                receive(level, sign, total)
        pair_receive(level, 3)
        pair_receive(level, far)

    def wait_sent(level):
        for total in range(1, far + 1):
            for sign in (1, -1):
                for i in range(count(total)):
                    sending(level, sign, total, i).wait_send()
                for i in range(count(total) if total == far else 1):
                    pair_copy(level, sign, total, i, True).wait_send()
        pair_block(level, True).wait_send()

    def load_isometry(level):
        pairs = iso_ref.shape[2] // 128
        for n in range(rows_own):
            for j in range(pairs):
                spread[n * pairs + j : n * pairs + j + 1, :] = iso_ref[level, n : n + 1, j * 128 : (j + 1) * 128]
        for n in range(rows_own):
            both = spread[n * pairs : (n + 1) * pairs, :]
            rows[pl.ds(n * 2 * pairs, pairs, stride=2), :] = both
            rows[pl.ds(n * 2 * pairs + 1, pairs, stride=2), :] = pltpu.roll(both, 64, 1)
        hi, lo = split(rows[...][:, :64])
        left_op[0, :, :64] = hi
        left_op[0, :, 64:] = hi
        left_op[1, :, :64] = lo

    low_lanes = lax.broadcasted_iota(jnp.int32, (64, 128), 1) < 64
    low_rows = lax.broadcasted_iota(jnp.int32, (8, 128), 0) < 4

    def contract(level, inverse):
        left_now = jnp.concatenate([left_op[0], left_op[1, :, :64]], axis=1)

        def first(i, _):
            lanes = pl.ds(pl.multiple_of(i * 128, 128), 128)
            top, bottom = [], []
            for d in range(0, parts, 2):
                x, y = gathered[level, d, :, lanes], gathered[level, d + 1, :, lanes]
                top.append(jnp.where(low_rows, x, pltpu.roll(y, 4, 0)))
                bottom.append(jnp.where(low_rows, pltpu.roll(x, 4, 0), y))
            both = jnp.concatenate(top + bottom, axis=0)
            if inverse is not None:
                both = both * inverse
            flipped[pl.ds(pl.multiple_of(i * 128, 128), 128), :] = both.T
            hi, lo = split(both)
            operand = jnp.concatenate(
                [jnp.concatenate([hi[h * 64 : h * 64 + 64], lo[h * 64 : h * 64 + 64], hi[h * 64 : h * 64 + 64]], axis=0) for h in (0, 1)],
                axis=1,
            )
            inner = jnp.dot(left_now, operand, preferred_element_type=F32)
            for h in (0, 1):
                for n in range(0, rows_own, 2):
                    x = inner[n * 64 : n * 64 + 64, h * 128 : h * 128 + 128]
                    y = inner[n * 64 + 64 : n * 64 + 128, h * 128 : h * 128 + 128]
                    for b, block in enumerate(interleave(x, y, low_lanes)):
                        place = pl.ds(pl.multiple_of(h * 2048 + i * 128, 128) + b * 64, 64)
                        hi, lo = split(block)
                        inner_hi[n // 2, place, :] = hi
                        inner_lo[n // 2, place, :] = lo
            return 0

        lax.fori_loop(0, half // 128, first, 0, unroll=UNROLL)

        low32 = low_lanes[:32]
        for j in range(32):
            x = flipped[pl.ds(2 * j, 32, stride=64), :]
            y = flipped[pl.ds(2 * j + 1, 32, stride=64), :]
            block = jnp.concatenate(interleave(x, y, low32), axis=0)
            hi, lo = split(block)
            weights[j, :64, :] = hi
            weights[j, 64:, :] = lo

        both = jnp.concatenate([weights[j] for j in range(32)], axis=1)
        main = jnp.dot(both, jnp.concatenate([inner_hi[0], inner_hi[1]], axis=1), preferred_element_type=F32)
        rest = jnp.dot(both[:64], jnp.concatenate([inner_lo[0], inner_lo[1]], axis=1), preferred_element_type=F32)
        return main[:64] + (main[64:] + rest)

    def own_layout(summed):
        rows[:64, :] = summed[:, :128]
        rows[64:128, :] = summed[:, 128:]
        for g in (0, 1):
            x = rows[pl.ds(g * 64, 32, stride=2), :]
            y = rows[pl.ds(g * 64 + 1, 32, stride=2), :]
            for b, block in enumerate(interleave(x, y, low_lanes[:32])):
                n = 2 * g + b
                turned[n * 16 : n * 16 + 16, :] = block[:16]
                turned[64 + n * 16 : 64 + n * 16 + 16, :] = block[16:]
        return [turned[pl.ds(j, 8, stride=16), :] for j in range(16)]

    def peak_over(level, offsets, peak):
        peaks = [peak] * 4
        for offset in offsets:
            for c in (0, 1):
                block = jnp.abs(gathered[level, slot_of(offset, c)])
                for j in range(half // 128):
                    peaks[j % 4] = jnp.maximum(peaks[j % 4], block[:, j * 128 : j * 128 + 128])
        return jnp.maximum(jnp.maximum(peaks[0], peaks[1]), jnp.maximum(peaks[2], peaks[3]))

    tensor_in.wait()
    gathered[0, me] = jnp.concatenate([tensor_ref[:, :half], tensor_ref[:, half:]], axis=0)
    pl.semaphore_wait(barrier, len(peers))
    start_gather(0)
    iso_in.wait()
    log_density = jnp.zeros((1, 1), F32)
    for level in range(levels):
        load_isometry(level)
        near_gather(level)
        peak = jnp.zeros((8, 128), F32)
        if level > 0:
            peak = peak_over(level, range(-2, 3), peak)
        far_gather(level)
        inverse = None
        if level > 0:
            peak = peak_over(level, range(3, 6), peak)
            largest = jnp.max(jnp.max(peak, axis=0, keepdims=True), axis=1, keepdims=True) + EPSILON
            log_density = log_density + jnp.log(largest) * 0.5**level
            inverse = 1.0 / largest
        tiles = own_layout(contract(level, inverse))
        if level + 1 < levels:
            for j, tile in enumerate(tiles):
                gathered[level + 1, me, :, j * 128 : j * 128 + 128] = tile
            start_gather(level + 1)

    peak = functools.reduce(jnp.maximum, [jnp.abs(tile) for tile in tiles])
    peak = jnp.max(peak, axis=0, keepdims=True)
    own_peak[...] = peak
    peaks[me] = peak

    def peak_copy(d):
        return pltpu.make_async_remote_copy(
            src_ref=own_peak,
            dst_ref=peaks.at[me],
            send_sem=peak_send.at[d],
            recv_sem=peak_recv.at[d],
            device_id={"bond": lax.rem(me + d, parts)},
            device_id_type=pl.DeviceIdType.MESH,
        )

    def peak_arrival(d):
        return pltpu.make_async_remote_copy(
            src_ref=own_peak,
            dst_ref=peaks.at[lax.rem(me + parts - d, parts)],
            send_sem=peak_send.at[d],
            recv_sem=peak_recv.at[d],
            device_id={"bond": lax.rem(me + d, parts)},
            device_id_type=pl.DeviceIdType.MESH,
        )

    for d in range(1, parts):
        peak_copy(d).start()
    for level in range(levels):
        wait_sent(level)
    for d in range(1, parts):
        peak_arrival(d).wait_recv()
    peak = functools.reduce(jnp.maximum, [peaks[d] for d in range(parts)])
    largest = jnp.max(peak, axis=1, keepdims=True) + EPSILON
    log_density = log_density + jnp.log(largest) * 0.5**levels
    inverse = 1.0 / largest
    for j, tile in enumerate(tiles):
        tile = tile * inverse
        out_ref[:, j * 128 : j * 128 + 128] = tile[:4]
        out_ref[:, half + j * 128 : half + j * 128 + 128] = tile[4:]
    log_ref[...] = jnp.broadcast_to(log_density, log_ref.shape)
    for d in range(1, parts):
        peak_copy(d).wait_send()


def solution(mesh):
    parts = mesh.shape["bond"]

    def on_device(tensor, isometries):
        levels = isometries.shape[0]
        rows, width2 = tensor.shape
        width = rows * parts
        far = parts // 4
        dma = pltpu.SemaphoreType.DMA
        vmem = pl.BlockSpec(memory_space=pltpu.VMEM)
        out, log_density = pl.pallas_call(
            functools.partial(kernel, levels, parts),
            out_shape=(jax.ShapeDtypeStruct(tensor.shape, F32), jax.ShapeDtypeStruct((1, 128), F32)),
            in_specs=[pl.BlockSpec(memory_space=pl.ANY)] * 2,
            out_specs=(vmem, vmem),
            scratch_shapes=[
                pltpu.VMEM(tensor.shape, F32),
                pltpu.VMEM(isometries.shape, F32),
                pltpu.VMEM((levels, parts, 2 * rows, width2 // 2), F32),
                pltpu.VMEM((parts, 1, 128), F32),
                pltpu.VMEM((1, 128), F32),
                pltpu.VMEM((rows * width // 2, 128), F32),
                pltpu.VMEM((rows * width, 128), F32),
                pltpu.VMEM((width // 2, 2 * width, 128), BF16),
                pltpu.VMEM((width2 // 2, 128), F32),
                pltpu.VMEM((2, rows * width, 128), BF16),
                pltpu.VMEM((rows // 2, width2, 128), BF16),
                pltpu.VMEM((rows // 2, width2, 128), BF16),
                pltpu.VMEM((128, 128), F32),
                dma((levels, far, 2, PIECES)),
                dma((levels, far, 2, PIECES)),
                dma((levels, far + 1, 2, PIECES)),
                dma((levels, far + 1, 2, PIECES)),
                dma((parts,)),
                dma((parts,)),
                dma((2,)),
            ],
            compiler_params=pltpu.CompilerParams(collective_id=0, has_side_effects=True),
        )(tensor, isometries)
        return out, log_density[0, :1]

    in_specs = (P(("temp", "bond"), None), P("temp", "bond", None))
    out_specs = (P(("temp", "bond"), None), P("temp"))
    return jax.shard_map(on_device, mesh=mesh, in_specs=in_specs, out_specs=out_specs, check_vma=False)
```

```python
import functools

import jax
import jax.numpy as jnp
from jax import lax
from jax.experimental import pallas as pl
from jax.experimental.pallas import tpu as pltpu
from jax.sharding import PartitionSpec as P

EPSILON = 1e-06
PIECES = 2
UNROLL = 8
F32 = jnp.float32
BF16 = jnp.bfloat16


def split(x):
    high = x.astype(BF16)
    return high, (x - high.astype(F32)).astype(BF16)


def interleave(x, y, low):
    kept = jnp.where(low, x, y)
    moved = pltpu.roll(jnp.where(low, y, x), 64, 1)
    return jnp.where(low, kept, moved), jnp.where(low, moved, kept)


def kernel(
    levels, parts, tensor_hbm, iso_hbm, out_ref, log_ref,
    tensor_ref, iso_ref, gathered, peaks, own_peak, spread, rows, weights, flipped, left_op, inner_hi, inner_lo, turned,
    ring_recv, pair_recv, sent_sem, peak_send, peak_recv, in_sem,
):
    tensor_in = pltpu.make_async_copy(tensor_hbm, tensor_ref, in_sem.at[0])
    iso_in = pltpu.make_async_copy(iso_hbm, iso_ref, in_sem.at[1])
    tensor_in.start()
    iso_in.start()
    me = lax.axis_index("bond")
    core = lax.rem(me, 2)
    chip = me // 2
    chips = parts // 2
    far = chips // 2
    rows_own, width2 = tensor_ref.shape
    half = width2 // 2
    wide = half // PIECES

    def slot_of(offset, core):
        return lax.rem(chip + offset + chips, chips) * 2 + core

    pair = chip * 2 + (1 - core)
    signs = (1 - 2 * (chip < 2).astype(jnp.int32), 2 * (chip < 2).astype(jnp.int32) - 1)

    peers = [slot_of(offset, core) for offset in (1, -1, 2, -2)] + [pair]
    barrier = pltpu.get_barrier_semaphore()
    for peer in peers:
        pl.semaphore_signal(barrier, inc=1, device_id={"bond": peer}, device_id_type=pl.DeviceIdType.MESH)

    def lanes_of(sign, i):
        q = lax.rem(i + way_of(sign) * (PIECES // 2), PIECES)
        return pl.ds(q * wide if isinstance(q, int) else pl.multiple_of(q * wide, 128), wide)

    def remote(ref, send_sem, recv_sem, device):
        return pltpu.make_async_remote_copy(
            src_ref=ref,
            dst_ref=ref,
            send_sem=send_sem,
            recv_sem=recv_sem,
            device_id={"bond": device},
            device_id_type=pl.DeviceIdType.MESH,
        )

    def way_of(sign):
        return (1 - sign) // 2

    def ring_copy(level, sign, total, hops, i, offset):
        ref = gathered.at[level, slot_of(offset, core)]
        if total in (2, far):
            ref = ref.at[:, lanes_of(sign, i)]
        way = way_of(sign)
        place = (0, 1, 3, 4)[total - 1] + i
        return remote(ref, sent_sem.at[level], ring_recv.at[level, way, place], slot_of(sign * hops, core))

    def sending(level, sign, total, i):
        hops = total if total <= 2 else total - 2
        return ring_copy(level, sign, total, hops, i, sign * (hops - total))

    def arriving(level, sign, total, i):
        return ring_copy(level, sign, total, total if total <= 2 else total - 2, i, -sign * total)

    def count(total):
        return PIECES // 2 if total == far else PIECES if total == 2 else 1

    def pair_copy(level, sign, total, i, sent):
        slot = slot_of(-sign * total, core if sent else 1 - core)
        ref = gathered.at[level, slot]
        if total == far:
            ref = ref.at[:, lanes_of(sign, i)]
        return remote(ref, sent_sem.at[level], pair_recv.at[level, total // 3], pair)

    def pair_block(level, sent):
        ref = gathered.at[level, me if sent else pair]
        return remote(ref, sent_sem.at[level], pair_recv.at[level, 0], pair)

    def start_gather(level):
        for total in (2, 1):
            for i in range(count(total)):
                for sign in (1, -1):
                    sending(level, sign, total, i).start()
        pair_block(level, True).start()

    def receive(level, sign, total):
        for i in range(count(total)):
            arriving(level, sign, total, i).wait_recv()
            pair_copy(level, sign, total, i, True).start()

    def pair_receive(level, part):
        blocks = gathered.at[level, pl.ds(0, (5, 3)[part])]
        remote(blocks, sent_sem.at[level], pair_recv.at[level, part], pair).wait_recv()

    def near_gather(level):
        for sign in signs:
            for i in range(PIECES):
                arriving(level, sign, 2, i).wait_recv()
                if i < count(far):
                    sending(level, sign, far, i).start()
            sending(level, sign, 3, 0).start()
            pair_copy(level, sign, 2, 0, True).start()
        for sign in signs:
            receive(level, sign, 1)
        pair_receive(level, 0)

    def far_gather(level):
        for total in (far, 3):
            for sign in signs:
                receive(level, sign, total)
        pair_receive(level, 1)

    def wait_sent(level):
        blocks = gathered.at[level, pl.ds(0, 15)]
        remote(blocks, sent_sem.at[level], pair_recv.at[level, 0], pair).wait_send()

    def load_isometry(level):
        pairs = iso_ref.shape[2] // 128
        for n in range(rows_own):
            for j in range(pairs):
                spread[n * pairs + j : n * pairs + j + 1, :] = iso_ref[level, n : n + 1, j * 128 : (j + 1) * 128]
        for n in range(rows_own):
            both = spread[n * pairs : (n + 1) * pairs, :]
            rows[pl.ds(n * 2 * pairs, pairs, stride=2), :] = both
            rows[pl.ds(n * 2 * pairs + 1, pairs, stride=2), :] = pltpu.roll(both, 64, 1)
        hi, lo = split(rows[...][:, :64])
        left_op[0, :, :64] = hi
        left_op[0, :, 64:] = hi
        left_op[1, :, :64] = lo

    low_lanes = lax.broadcasted_iota(jnp.int32, (64, 128), 1) < 64
    low_rows = lax.broadcasted_iota(jnp.int32, (8, 128), 0) < 4

    def contract(level, inverse):
        left_now = jnp.concatenate([left_op[0], left_op[1, :, :64]], axis=1)

        def first(i, _):
            lanes = pl.ds(pl.multiple_of(i * 128, 128), 128)
            top, bottom = [], []
            for d in range(0, parts, 2):
                x, y = gathered[level, d, :, lanes], gathered[level, d + 1, :, lanes]
                top.append(jnp.where(low_rows, x, pltpu.roll(y, 4, 0)))
                bottom.append(jnp.where(low_rows, pltpu.roll(x, 4, 0), y))
            both = jnp.concatenate(top + bottom, axis=0)
            if inverse is not None:
                both = both * inverse
            flipped[pl.ds(pl.multiple_of(i * 128, 128), 128), :] = both.T
            hi, lo = split(both)
            operand = jnp.concatenate(
                [jnp.concatenate([hi[h * 64 : h * 64 + 64], lo[h * 64 : h * 64 + 64], hi[h * 64 : h * 64 + 64]], axis=0) for h in (0, 1)],
                axis=1,
            )
            inner = jnp.dot(left_now, operand, preferred_element_type=F32)
            for h in (0, 1):
                for n in range(0, rows_own, 2):
                    x = inner[n * 64 : n * 64 + 64, h * 128 : h * 128 + 128]
                    y = inner[n * 64 + 64 : n * 64 + 128, h * 128 : h * 128 + 128]
                    for b, block in enumerate(interleave(x, y, low_lanes)):
                        place = pl.ds(pl.multiple_of(h * 2048 + i * 128, 128) + b * 64, 64)
                        hi, lo = split(block)
                        inner_hi[n // 2, place, :] = hi
                        inner_lo[n // 2, place, :] = lo
            return 0

        lax.fori_loop(0, half // 128, first, 0, unroll=UNROLL)

        low32 = low_lanes[:32]
        for j in range(32):
            x = flipped[pl.ds(2 * j, 32, stride=64), :]
            y = flipped[pl.ds(2 * j + 1, 32, stride=64), :]
            block = jnp.concatenate(interleave(x, y, low32), axis=0)
            hi, lo = split(block)
            weights[j, :64, :] = hi
            weights[j, 64:, :] = lo

        both = jnp.concatenate([weights[j] for j in range(32)], axis=1)
        main = jnp.dot(both, jnp.concatenate([inner_hi[0], inner_hi[1]], axis=1), preferred_element_type=F32)
        rest = jnp.dot(both[:64], jnp.concatenate([inner_lo[0], inner_lo[1]], axis=1), preferred_element_type=F32)
        return main[:64] + (main[64:] + rest)

    def own_layout(summed):
        rows[:64, :] = summed[:, :128]
        rows[64:128, :] = summed[:, 128:]
        for g in (0, 1):
            x = rows[pl.ds(g * 64, 32, stride=2), :]
            y = rows[pl.ds(g * 64 + 1, 32, stride=2), :]
            for b, block in enumerate(interleave(x, y, low_lanes[:32])):
                n = 2 * g + b
                turned[n * 16 : n * 16 + 16, :] = block[:16]
                turned[64 + n * 16 : 64 + n * 16 + 16, :] = block[16:]
        return [turned[pl.ds(j, 8, stride=16), :] for j in range(16)]

    def peak_over(level, offsets, peak):
        peaks = [peak] * 4
        for offset in offsets:
            for c in (0, 1):
                block = jnp.abs(gathered[level, slot_of(offset, c)])
                for j in range(half // 128):
                    peaks[j % 4] = jnp.maximum(peaks[j % 4], block[:, j * 128 : j * 128 + 128])
        return jnp.maximum(jnp.maximum(peaks[0], peaks[1]), jnp.maximum(peaks[2], peaks[3]))

    tensor_in.wait()
    gathered[0, me] = jnp.concatenate([tensor_ref[:, :half], tensor_ref[:, half:]], axis=0)
    pl.semaphore_wait(barrier, len(peers))
    start_gather(0)
    iso_in.wait()
    log_density = jnp.zeros((1, 1), F32)
    for level in range(levels):
        load_isometry(level)
        near_gather(level)
        peak = jnp.zeros((8, 128), F32)
        if level > 0:
            peak = peak_over(level, range(-2, 3), peak)
        far_gather(level)
        inverse = None
        if level > 0:
            peak = peak_over(level, range(3, 6), peak)
            largest = jnp.max(jnp.max(peak, axis=0, keepdims=True), axis=1, keepdims=True) + EPSILON
            log_density = log_density + jnp.log(largest) * 0.5**level
            inverse = 1.0 / largest
        tiles = own_layout(contract(level, inverse))
        if level + 1 < levels:
            for j, tile in enumerate(tiles):
                gathered[level + 1, me, :, j * 128 : j * 128 + 128] = tile
            start_gather(level + 1)

    peak = functools.reduce(jnp.maximum, [jnp.abs(tile) for tile in tiles])
    peak = jnp.max(peak, axis=0, keepdims=True)
    own_peak[0] = peak
    peaks[me] = peak

    def peak_copy(src, dst, d):
        return pltpu.make_async_remote_copy(
            src_ref=src,
            dst_ref=dst,
            send_sem=peak_send.at[0],
            recv_sem=peak_recv.at[0],
            device_id={"bond": lax.rem(me + d, parts)},
            device_id_type=pl.DeviceIdType.MESH,
        )

    for d in sorted(range(1, parts), key=lambda d: -min(d, parts - d)):
        peak_copy(own_peak.at[0], peaks.at[me], d).start()
    others = peaks.at[pl.ds(0, parts - 1)]
    peak_copy(others, others, 1).wait_send()
    for level in range(levels):
        wait_sent(level)
    peak_copy(others, others, 1).wait_recv()
    peak = functools.reduce(jnp.maximum, [peaks[d] for d in range(parts)])
    largest = jnp.max(peak, axis=1, keepdims=True) + EPSILON
    log_density = log_density + jnp.log(largest) * 0.5**levels
    inverse = 1.0 / largest
    for j, tile in enumerate(tiles):
        tile = tile * inverse
        out_ref[:, j * 128 : j * 128 + 128] = tile[:4]
        out_ref[:, half + j * 128 : half + j * 128 + 128] = tile[4:]
    log_ref[...] = jnp.broadcast_to(log_density, log_ref.shape)


def solution(mesh):
    parts = mesh.shape["bond"]

    def on_device(tensor, isometries):
        levels = isometries.shape[0]
        rows, width2 = tensor.shape
        width = rows * parts
        far = parts // 4
        dma = pltpu.SemaphoreType.DMA
        vmem = pl.BlockSpec(memory_space=pltpu.VMEM)
        out, log_density = pl.pallas_call(
            functools.partial(kernel, levels, parts),
            out_shape=(jax.ShapeDtypeStruct(tensor.shape, F32), jax.ShapeDtypeStruct((1, 128), F32)),
            in_specs=[pl.BlockSpec(memory_space=pl.ANY)] * 2,
            out_specs=(vmem, vmem),
            scratch_shapes=[
                pltpu.VMEM(tensor.shape, F32),
                pltpu.VMEM(isometries.shape, F32),
                pltpu.VMEM((levels, parts, 2 * rows, width2 // 2), F32),
                pltpu.VMEM((parts, 1, 128), F32),
                pltpu.VMEM((1, 1, 128), F32),
                pltpu.VMEM((rows * width // 2, 128), F32),
                pltpu.VMEM((rows * width, 128), F32),
                pltpu.VMEM((width // 2, 2 * width, 128), BF16),
                pltpu.VMEM((width2 // 2, 128), F32),
                pltpu.VMEM((2, rows * width, 128), BF16),
                pltpu.VMEM((rows // 2, width2, 128), BF16),
                pltpu.VMEM((rows // 2, width2, 128), BF16),
                pltpu.VMEM((128, 128), F32),
                dma((levels, 2, far + 1)),
                dma((levels, 2)),
                dma((levels,)),
                dma((1,)),
                dma((1,)),
                dma((2,)),
            ],
            compiler_params=pltpu.CompilerParams(collective_id=0, has_side_effects=True),
        )(tensor, isometries)
        return out, log_density[0, :1]

    in_specs = (P(("temp", "bond"), None), P("temp", "bond", None))
    out_specs = (P(("temp", "bond"), None), P("temp"))
    return jax.shard_map(on_device, mesh=mesh, in_specs=in_specs, out_specs=out_specs, check_vma=False)
```

```python
import functools

import jax
import jax.numpy as jnp
from jax import lax
from jax.experimental import pallas as pl
from jax.experimental.pallas import tpu as pltpu
from jax.sharding import PartitionSpec as P

EPSILON = 1e-06
PIECES = 2
UNROLL = 8
F32 = jnp.float32
BF16 = jnp.bfloat16


def split(x):
    high = x.astype(BF16)
    return high, (x - high.astype(F32)).astype(BF16)


def interleave(x, y, low):
    kept = jnp.where(low, x, y)
    moved = pltpu.roll(jnp.where(low, y, x), 64, 1)
    return jnp.where(low, kept, moved), jnp.where(low, moved, kept)


def kernel(
    levels, parts, tensor_hbm, iso_hbm, out_ref, log_ref,
    tensor_ref, iso_ref, gathered, peaks, own_peak, spread, rows, weights, flipped, left_op, inner_hi, inner_lo, turned,
    ring_recv, pair_recv, sent_sem, peak_send, peak_recv, in_sem,
):
    tensor_in = pltpu.make_async_copy(tensor_hbm, tensor_ref, in_sem.at[0])
    iso_in = pltpu.make_async_copy(iso_hbm, iso_ref, in_sem.at[1])
    tensor_in.start()
    iso_in.start()
    me = lax.axis_index("bond")
    core = lax.rem(me, 2)
    chip = me // 2
    chips = parts // 2
    far = chips // 2
    rows_own, width2 = tensor_ref.shape
    half = width2 // 2
    wide = half // PIECES

    def slot_of(offset, core):
        return lax.rem(chip + offset + chips, chips) * 2 + core

    pair = chip * 2 + (1 - core)
    signs = (1 - 2 * (chip < 2).astype(jnp.int32), 2 * (chip < 2).astype(jnp.int32) - 1)

    peers = [slot_of(offset, core) for offset in (1, -1, 2, -2)] + [pair]
    barrier = pltpu.get_barrier_semaphore()
    for peer in peers:
        pl.semaphore_signal(barrier, inc=1, device_id={"bond": peer}, device_id_type=pl.DeviceIdType.MESH)

    def lanes_of(sign, i):
        q = lax.rem(i + way_of(sign) * (PIECES // 2), PIECES)
        return pl.ds(q * wide if isinstance(q, int) else pl.multiple_of(q * wide, 128), wide)

    def remote(ref, send_sem, recv_sem, device):
        return pltpu.make_async_remote_copy(
            src_ref=ref,
            dst_ref=ref,
            send_sem=send_sem,
            recv_sem=recv_sem,
            device_id={"bond": device},
            device_id_type=pl.DeviceIdType.MESH,
        )

    def way_of(sign):
        return (1 - sign) // 2

    def ring_copy(level, sign, total, hops, i, offset):
        ref = gathered.at[level, slot_of(offset, core)]
        if total > 1:
            ref = ref.at[:, lanes_of(sign, i)]
        way = way_of(sign)
        place = (0, 1, 1 + PIECES, 1 + 2 * PIECES)[total - 1] + i
        return remote(ref, sent_sem.at[level], ring_recv.at[level, way, place], slot_of(sign * hops, core))

    def sending(level, sign, total, i):
        hops = total if total <= 2 else total - 2
        return ring_copy(level, sign, total, hops, i, sign * (hops - total))

    def arriving(level, sign, total, i):
        return ring_copy(level, sign, total, total if total <= 2 else total - 2, i, -sign * total)

    def count(total):
        return PIECES // 2 if total == far else 1 if total == 1 else PIECES

    def pair_copy(level, sign, total, i, sent):
        slot = slot_of(-sign * total, core if sent else 1 - core)
        ref = gathered.at[level, slot]
        if total > 2:
            ref = ref.at[:, lanes_of(sign, i)]
        return remote(ref, sent_sem.at[level], pair_recv.at[level, total // 3], pair)

    def pair_block(level, sent):
        ref = gathered.at[level, me if sent else pair]
        return remote(ref, sent_sem.at[level], pair_recv.at[level, 0], pair)

    def start_gather(level):
        for total in (2, 1):
            for i in range(count(total)):
                for sign in (1, -1):
                    sending(level, sign, total, i).start()
        pair_block(level, True).start()

    def receive(level, sign, total):
        for i in range(count(total)):
            arriving(level, sign, total, i).wait_recv()
            pair_copy(level, sign, total, i, True).start()

    def pair_receive(level, part):
        blocks = gathered.at[level, pl.ds(0, (5, 3)[part])]
        remote(blocks, sent_sem.at[level], pair_recv.at[level, part], pair).wait_recv()

    def near_gather(level):
        for sign in signs:
            for i in range(PIECES):
                arriving(level, sign, 2, i).wait_recv()
                if i < count(far):
                    sending(level, sign, far, i).start()
                sending(level, sign, 3, i).start()
            pair_copy(level, sign, 2, 0, True).start()
        for sign in signs:
            receive(level, sign, 1)
        pair_receive(level, 0)

    def far_gather(level):
        for total in (far, 3):
            for sign in signs:
                receive(level, sign, total)
        pair_receive(level, 1)

    def wait_sent(level):
        blocks = gathered.at[level, pl.ds(0, 15)]
        remote(blocks, sent_sem.at[level], pair_recv.at[level, 0], pair).wait_send()

    def load_isometry(level):
        pairs = iso_ref.shape[2] // 128
        for n in range(rows_own):
            for j in range(pairs):
                spread[n * pairs + j : n * pairs + j + 1, :] = iso_ref[level, n : n + 1, j * 128 : (j + 1) * 128]
        for n in range(rows_own):
            both = spread[n * pairs : (n + 1) * pairs, :]
            rows[pl.ds(n * 2 * pairs, pairs, stride=2), :] = both
            rows[pl.ds(n * 2 * pairs + 1, pairs, stride=2), :] = pltpu.roll(both, 64, 1)
        hi, lo = split(rows[...][:, :64])
        left_op[0, :, :64] = hi
        left_op[0, :, 64:] = hi
        left_op[1, :, :64] = lo

    low_lanes = lax.broadcasted_iota(jnp.int32, (64, 128), 1) < 64
    low_rows = lax.broadcasted_iota(jnp.int32, (8, 128), 0) < 4

    def contract(level, inverse):
        left_now = jnp.concatenate([left_op[0], left_op[1, :, :64]], axis=1)

        def first(i, _):
            lanes = pl.ds(pl.multiple_of(i * 128, 128), 128)
            top, bottom = [], []
            for d in range(0, parts, 2):
                x, y = gathered[level, d, :, lanes], gathered[level, d + 1, :, lanes]
                top.append(jnp.where(low_rows, x, pltpu.roll(y, 4, 0)))
                bottom.append(jnp.where(low_rows, pltpu.roll(x, 4, 0), y))
            both = jnp.concatenate(top + bottom, axis=0)
            if inverse is not None:
                both = both * inverse
            flipped[pl.ds(pl.multiple_of(i * 128, 128), 128), :] = both.T
            hi, lo = split(both)
            operand = jnp.concatenate(
                [jnp.concatenate([hi[h * 64 : h * 64 + 64], lo[h * 64 : h * 64 + 64], hi[h * 64 : h * 64 + 64]], axis=0) for h in (0, 1)],
                axis=1,
            )
            inner = jnp.dot(left_now, operand, preferred_element_type=F32)
            for h in (0, 1):
                for n in range(0, rows_own, 2):
                    x = inner[n * 64 : n * 64 + 64, h * 128 : h * 128 + 128]
                    y = inner[n * 64 + 64 : n * 64 + 128, h * 128 : h * 128 + 128]
                    for b, block in enumerate(interleave(x, y, low_lanes)):
                        place = pl.ds(pl.multiple_of(h * 2048 + i * 128, 128) + b * 64, 64)
                        hi, lo = split(block)
                        inner_hi[n // 2, place, :] = hi
                        inner_lo[n // 2, place, :] = lo
            return 0

        lax.fori_loop(0, half // 128, first, 0, unroll=UNROLL)

        low32 = low_lanes[:32]
        for j in range(32):
            x = flipped[pl.ds(2 * j, 32, stride=64), :]
            y = flipped[pl.ds(2 * j + 1, 32, stride=64), :]
            block = jnp.concatenate(interleave(x, y, low32), axis=0)
            hi, lo = split(block)
            weights[j, :64, :] = hi
            weights[j, 64:, :] = lo

        both = jnp.concatenate([weights[j] for j in range(32)], axis=1)
        main = jnp.dot(both, jnp.concatenate([inner_hi[0], inner_hi[1]], axis=1), preferred_element_type=F32)
        rest = jnp.dot(both[:64], jnp.concatenate([inner_lo[0], inner_lo[1]], axis=1), preferred_element_type=F32)
        return main[:64] + (main[64:] + rest)

    def own_layout(summed):
        rows[:64, :] = summed[:, :128]
        rows[64:128, :] = summed[:, 128:]
        for g in (0, 1):
            x = rows[pl.ds(g * 64, 32, stride=2), :]
            y = rows[pl.ds(g * 64 + 1, 32, stride=2), :]
            for b, block in enumerate(interleave(x, y, low_lanes[:32])):
                n = 2 * g + b
                turned[n * 16 : n * 16 + 16, :] = block[:16]
                turned[64 + n * 16 : 64 + n * 16 + 16, :] = block[16:]
        return [turned[pl.ds(j, 8, stride=16), :] for j in range(16)]

    def peak_over(level, offsets, peak):
        peaks = [peak] * 4
        for offset in offsets:
            for c in (0, 1):
                block = jnp.abs(gathered[level, slot_of(offset, c)])
                for j in range(half // 128):
                    peaks[j % 4] = jnp.maximum(peaks[j % 4], block[:, j * 128 : j * 128 + 128])
        return jnp.maximum(jnp.maximum(peaks[0], peaks[1]), jnp.maximum(peaks[2], peaks[3]))

    tensor_in.wait()
    gathered[0, me] = jnp.concatenate([tensor_ref[:, :half], tensor_ref[:, half:]], axis=0)
    pl.semaphore_wait(barrier, len(peers))
    start_gather(0)
    iso_in.wait()
    log_density = jnp.zeros((1, 1), F32)
    for level in range(levels):
        load_isometry(level)
        near_gather(level)
        peak = jnp.zeros((8, 128), F32)
        if level > 0:
            peak = peak_over(level, range(-2, 3), peak)
        far_gather(level)
        inverse = None
        if level > 0:
            peak = peak_over(level, range(3, 6), peak)
            largest = jnp.max(jnp.max(peak, axis=0, keepdims=True), axis=1, keepdims=True) + EPSILON
            log_density = log_density + jnp.log(largest) * 0.5**level
            inverse = 1.0 / largest
        tiles = own_layout(contract(level, inverse))
        if level + 1 < levels:
            for j, tile in enumerate(tiles):
                gathered[level + 1, me, :, j * 128 : j * 128 + 128] = tile
            start_gather(level + 1)

    peak = functools.reduce(jnp.maximum, [jnp.abs(tile) for tile in tiles])
    peak = jnp.max(peak, axis=0, keepdims=True)
    own_peak[0] = peak
    peaks[me] = peak

    def peak_copy(src, dst, d):
        return pltpu.make_async_remote_copy(
            src_ref=src,
            dst_ref=dst,
            send_sem=peak_send.at[0],
            recv_sem=peak_recv.at[0],
            device_id={"bond": lax.rem(me + d, parts)},
            device_id_type=pl.DeviceIdType.MESH,
        )

    for d in sorted(range(1, parts), key=lambda d: -min(d, parts - d)):
        peak_copy(own_peak.at[0], peaks.at[me], d).start()
    others = peaks.at[pl.ds(0, parts - 1)]
    peak_copy(others, others, 1).wait_send()
    for level in range(levels):
        wait_sent(level)
    peak_copy(others, others, 1).wait_recv()
    peak = functools.reduce(jnp.maximum, [peaks[d] for d in range(parts)])
    largest = jnp.max(peak, axis=1, keepdims=True) + EPSILON
    log_density = log_density + jnp.log(largest) * 0.5**levels
    inverse = 1.0 / largest
    for j, tile in enumerate(tiles):
        tile = tile * inverse
        out_ref[:, j * 128 : j * 128 + 128] = tile[:4]
        out_ref[:, half + j * 128 : half + j * 128 + 128] = tile[4:]
    log_ref[...] = jnp.broadcast_to(log_density, log_ref.shape)


def solution(mesh):
    parts = mesh.shape["bond"]

    def on_device(tensor, isometries):
        levels = isometries.shape[0]
        rows, width2 = tensor.shape
        width = rows * parts
        far = parts // 4
        dma = pltpu.SemaphoreType.DMA
        vmem = pl.BlockSpec(memory_space=pltpu.VMEM)
        out, log_density = pl.pallas_call(
            functools.partial(kernel, levels, parts),
            out_shape=(jax.ShapeDtypeStruct(tensor.shape, F32), jax.ShapeDtypeStruct((1, 128), F32)),
            in_specs=[pl.BlockSpec(memory_space=pl.ANY)] * 2,
            out_specs=(vmem, vmem),
            scratch_shapes=[
                pltpu.VMEM(tensor.shape, F32),
                pltpu.VMEM(isometries.shape, F32),
                pltpu.VMEM((levels, parts, 2 * rows, width2 // 2), F32),
                pltpu.VMEM((parts, 1, 128), F32),
                pltpu.VMEM((1, 1, 128), F32),
                pltpu.VMEM((rows * width // 2, 128), F32),
                pltpu.VMEM((rows * width, 128), F32),
                pltpu.VMEM((width // 2, 2 * width, 128), BF16),
                pltpu.VMEM((width2 // 2, 128), F32),
                pltpu.VMEM((2, rows * width, 128), BF16),
                pltpu.VMEM((rows // 2, width2, 128), BF16),
                pltpu.VMEM((rows // 2, width2, 128), BF16),
                pltpu.VMEM((128, 128), F32),
                dma((levels, 2, 1 + 2 * PIECES + PIECES // 2)),
                dma((levels, 2)),
                dma((levels,)),
                dma((1,)),
                dma((1,)),
                dma((2,)),
            ],
            compiler_params=pltpu.CompilerParams(collective_id=0, has_side_effects=True),
        )(tensor, isometries)
        return out, log_density[0, :1]

    in_specs = (P(("temp", "bond"), None), P("temp", "bond", None))
    out_specs = (P(("temp", "bond"), None), P("temp"))
    return jax.shard_map(on_device, mesh=mesh, in_specs=in_specs, out_specs=out_specs, check_vma=False)
```

```python
import functools

import jax
import jax.numpy as jnp
from jax import lax
from jax.experimental import pallas as pl
from jax.experimental.pallas import tpu as pltpu
from jax.sharding import PartitionSpec as P

EPSILON = 1e-06
PIECES = 4
UNROLL = 8
F32 = jnp.float32
BF16 = jnp.bfloat16


def split(x):
    high = x.astype(BF16)
    return high, (x - high.astype(F32)).astype(BF16)


def interleave(x, y, low):
    kept = jnp.where(low, x, y)
    moved = pltpu.roll(jnp.where(low, y, x), 64, 1)
    return jnp.where(low, kept, moved), jnp.where(low, moved, kept)


def kernel(
    levels, parts, tensor_hbm, iso_hbm, out_ref, log_ref,
    tensor_ref, iso_ref, gathered, peaks, own_peak, spread, rows, weights, flipped, left_op, inner_hi, inner_lo, turned,
    ring_recv, pair_recv, sent_sem, peak_send, peak_recv, in_sem,
):
    tensor_in = pltpu.make_async_copy(tensor_hbm, tensor_ref, in_sem.at[0])
    iso_in = pltpu.make_async_copy(iso_hbm, iso_ref, in_sem.at[1])
    tensor_in.start()
    iso_in.start()
    me = lax.axis_index("bond")
    core = lax.rem(me, 2)
    chip = me // 2
    chips = parts // 2
    far = chips // 2
    rows_own, width2 = tensor_ref.shape
    half = width2 // 2
    wide = half // PIECES

    def slot_of(offset, core):
        return lax.rem(chip + offset + chips, chips) * 2 + core

    pair = chip * 2 + (1 - core)
    signs = (1 - 2 * (chip < 2).astype(jnp.int32), 2 * (chip < 2).astype(jnp.int32) - 1)

    peers = [slot_of(offset, core) for offset in (1, -1, 2, -2)] + [pair]
    barrier = pltpu.get_barrier_semaphore()
    for peer in peers:
        pl.semaphore_signal(barrier, inc=1, device_id={"bond": peer}, device_id_type=pl.DeviceIdType.MESH)

    def lanes_of(sign, i):
        q = lax.rem(i + way_of(sign) * (PIECES // 2), PIECES)
        return pl.ds(q * wide if isinstance(q, int) else pl.multiple_of(q * wide, 128), wide)

    def remote(ref, send_sem, recv_sem, device):
        return pltpu.make_async_remote_copy(
            src_ref=ref,
            dst_ref=ref,
            send_sem=send_sem,
            recv_sem=recv_sem,
            device_id={"bond": device},
            device_id_type=pl.DeviceIdType.MESH,
        )

    def way_of(sign):
        return (1 - sign) // 2

    def ring_copy(level, sign, total, hops, i, offset):
        ref = gathered.at[level, slot_of(offset, core)]
        if total > 1:
            ref = ref.at[:, lanes_of(sign, i)]
        way = way_of(sign)
        place = (0, 1, 1 + PIECES, 1 + 2 * PIECES)[total - 1] + i
        return remote(ref, sent_sem.at[level], ring_recv.at[level, way, place], slot_of(sign * hops, core))

    def sending(level, sign, total, i):
        hops = total if total <= 2 else total - 2
        return ring_copy(level, sign, total, hops, i, sign * (hops - total))

    def arriving(level, sign, total, i):
        return ring_copy(level, sign, total, total if total <= 2 else total - 2, i, -sign * total)

    def count(total):
        return PIECES // 2 if total == far else 1 if total == 1 else PIECES

    def pair_copy(level, sign, total, i, sent):
        slot = slot_of(-sign * total, core if sent else 1 - core)
        ref = gathered.at[level, slot]
        if total > 2:
            ref = ref.at[:, lanes_of(sign, i)]
        return remote(ref, sent_sem.at[level], pair_recv.at[level, total // 3], pair)

    def pair_block(level, sent):
        ref = gathered.at[level, me if sent else pair]
        return remote(ref, sent_sem.at[level], pair_recv.at[level, 0], pair)

    def start_gather(level):
        for total in (2, 1):
            for i in range(count(total)):
                for sign in (1, -1):
                    sending(level, sign, total, i).start()
        pair_block(level, True).start()

    def receive(level, sign, total):
        for i in range(count(total)):
            arriving(level, sign, total, i).wait_recv()
            pair_copy(level, sign, total, i, True).start()

    def pair_receive(level, part):
        blocks = gathered.at[level, pl.ds(0, (5, 3)[part])]
        remote(blocks, sent_sem.at[level], pair_recv.at[level, part], pair).wait_recv()

    def near_gather(level):
        for sign in signs:
            for i in range(PIECES):
                arriving(level, sign, 2, i).wait_recv()
                if i < count(far):
                    sending(level, sign, far, i).start()
                sending(level, sign, 3, i).start()
            pair_copy(level, sign, 2, 0, True).start()
        for sign in signs:
            receive(level, sign, 1)
        pair_receive(level, 0)

    def far_gather(level):
        for total in (far, 3):
            for sign in signs:
                receive(level, sign, total)
        pair_receive(level, 1)

    def wait_sent(level):
        blocks = gathered.at[level, pl.ds(0, 15)]
        remote(blocks, sent_sem.at[level], pair_recv.at[level, 0], pair).wait_send()

    def load_isometry(level):
        pairs = iso_ref.shape[2] // 128
        for n in range(rows_own):
            for j in range(pairs):
                spread[n * pairs + j : n * pairs + j + 1, :] = iso_ref[level, n : n + 1, j * 128 : (j + 1) * 128]
        for n in range(rows_own):
            both = spread[n * pairs : (n + 1) * pairs, :]
            rows[pl.ds(n * 2 * pairs, pairs, stride=2), :] = both
            rows[pl.ds(n * 2 * pairs + 1, pairs, stride=2), :] = pltpu.roll(both, 64, 1)
        hi, lo = split(rows[...][:, :64])
        left_op[0, :, :64] = hi
        left_op[0, :, 64:] = hi
        left_op[1, :, :64] = lo

    low_lanes = lax.broadcasted_iota(jnp.int32, (64, 128), 1) < 64
    low_rows = lax.broadcasted_iota(jnp.int32, (8, 128), 0) < 4

    def contract(level, inverse):
        left_now = jnp.concatenate([left_op[0], left_op[1, :, :64]], axis=1)

        def first(i, _):
            lanes = pl.ds(pl.multiple_of(i * 128, 128), 128)
            top, bottom = [], []
            for d in range(0, parts, 2):
                x, y = gathered[level, d, :, lanes], gathered[level, d + 1, :, lanes]
                top.append(jnp.where(low_rows, x, pltpu.roll(y, 4, 0)))
                bottom.append(jnp.where(low_rows, pltpu.roll(x, 4, 0), y))
            both = jnp.concatenate(top + bottom, axis=0)
            if inverse is not None:
                both = both * inverse
            flipped[pl.ds(pl.multiple_of(i * 128, 128), 128), :] = both.T
            hi, lo = split(both)
            operand = jnp.concatenate(
                [jnp.concatenate([hi[h * 64 : h * 64 + 64], lo[h * 64 : h * 64 + 64], hi[h * 64 : h * 64 + 64]], axis=0) for h in (0, 1)],
                axis=1,
            )
            inner = jnp.dot(left_now, operand, preferred_element_type=F32)
            for h in (0, 1):
                for n in range(0, rows_own, 2):
                    x = inner[n * 64 : n * 64 + 64, h * 128 : h * 128 + 128]
                    y = inner[n * 64 + 64 : n * 64 + 128, h * 128 : h * 128 + 128]
                    for b, block in enumerate(interleave(x, y, low_lanes)):
                        place = pl.ds(pl.multiple_of(h * 2048 + i * 128, 128) + b * 64, 64)
                        hi, lo = split(block)
                        inner_hi[n // 2, place, :] = hi
                        inner_lo[n // 2, place, :] = lo
            return 0

        lax.fori_loop(0, half // 128, first, 0, unroll=UNROLL)

        low32 = low_lanes[:32]
        for j in range(32):
            x = flipped[pl.ds(2 * j, 32, stride=64), :]
            y = flipped[pl.ds(2 * j + 1, 32, stride=64), :]
            block = jnp.concatenate(interleave(x, y, low32), axis=0)
            hi, lo = split(block)
            weights[j, :64, :] = hi
            weights[j, 64:, :] = lo

        both = jnp.concatenate([weights[j] for j in range(32)], axis=1)
        main = jnp.dot(both, jnp.concatenate([inner_hi[0], inner_hi[1]], axis=1), preferred_element_type=F32)
        rest = jnp.dot(both[:64], jnp.concatenate([inner_lo[0], inner_lo[1]], axis=1), preferred_element_type=F32)
        return main[:64] + (main[64:] + rest)

    def own_layout(summed):
        rows[:64, :] = summed[:, :128]
        rows[64:128, :] = summed[:, 128:]
        for g in (0, 1):
            x = rows[pl.ds(g * 64, 32, stride=2), :]
            y = rows[pl.ds(g * 64 + 1, 32, stride=2), :]
            for b, block in enumerate(interleave(x, y, low_lanes[:32])):
                n = 2 * g + b
                turned[n * 16 : n * 16 + 16, :] = block[:16]
                turned[64 + n * 16 : 64 + n * 16 + 16, :] = block[16:]
        return [turned[pl.ds(j, 8, stride=16), :] for j in range(16)]

    def peak_over(level, offsets, peak):
        peaks = [peak] * 4
        for offset in offsets:
            for c in (0, 1):
                block = jnp.abs(gathered[level, slot_of(offset, c)])
                for j in range(half // 128):
                    peaks[j % 4] = jnp.maximum(peaks[j % 4], block[:, j * 128 : j * 128 + 128])
        return jnp.maximum(jnp.maximum(peaks[0], peaks[1]), jnp.maximum(peaks[2], peaks[3]))

    tensor_in.wait()
    gathered[0, me] = jnp.concatenate([tensor_ref[:, :half], tensor_ref[:, half:]], axis=0)
    pl.semaphore_wait(barrier, len(peers))
    start_gather(0)
    iso_in.wait()
    log_density = jnp.zeros((1, 1), F32)
    for level in range(levels):
        load_isometry(level)
        near_gather(level)
        peak = jnp.zeros((8, 128), F32)
        if level > 0:
            peak = peak_over(level, range(-2, 3), peak)
        far_gather(level)
        inverse = None
        if level > 0:
            peak = peak_over(level, range(3, 6), peak)
            largest = jnp.max(jnp.max(peak, axis=0, keepdims=True), axis=1, keepdims=True) + EPSILON
            log_density = log_density + jnp.log(largest) * 0.5**level
            inverse = 1.0 / largest
        tiles = own_layout(contract(level, inverse))
        if level + 1 < levels:
            for j, tile in enumerate(tiles):
                gathered[level + 1, me, :, j * 128 : j * 128 + 128] = tile
            start_gather(level + 1)

    peak = functools.reduce(jnp.maximum, [jnp.abs(tile) for tile in tiles])
    peak = jnp.max(peak, axis=0, keepdims=True)
    own_peak[0] = peak
    peaks[me] = peak

    def peak_copy(src, dst, d):
        return pltpu.make_async_remote_copy(
            src_ref=src,
            dst_ref=dst,
            send_sem=peak_send.at[0],
            recv_sem=peak_recv.at[0],
            device_id={"bond": lax.rem(me + d, parts)},
            device_id_type=pl.DeviceIdType.MESH,
        )

    for d in sorted(range(1, parts), key=lambda d: -min(d, parts - d)):
        peak_copy(own_peak.at[0], peaks.at[me], d).start()
    others = peaks.at[pl.ds(0, parts - 1)]
    peak_copy(others, others, 1).wait_send()
    for level in range(levels):
        wait_sent(level)
    peak_copy(others, others, 1).wait_recv()
    peak = functools.reduce(jnp.maximum, [peaks[d] for d in range(parts)])
    largest = jnp.max(peak, axis=1, keepdims=True) + EPSILON
    log_density = log_density + jnp.log(largest) * 0.5**levels
    inverse = 1.0 / largest
    for j, tile in enumerate(tiles):
        tile = tile * inverse
        out_ref[:, j * 128 : j * 128 + 128] = tile[:4]
        out_ref[:, half + j * 128 : half + j * 128 + 128] = tile[4:]
    log_ref[...] = jnp.broadcast_to(log_density, log_ref.shape)


def solution(mesh):
    parts = mesh.shape["bond"]

    def on_device(tensor, isometries):
        levels = isometries.shape[0]
        rows, width2 = tensor.shape
        width = rows * parts
        far = parts // 4
        dma = pltpu.SemaphoreType.DMA
        vmem = pl.BlockSpec(memory_space=pltpu.VMEM)
        out, log_density = pl.pallas_call(
            functools.partial(kernel, levels, parts),
            out_shape=(jax.ShapeDtypeStruct(tensor.shape, F32), jax.ShapeDtypeStruct((1, 128), F32)),
            in_specs=[pl.BlockSpec(memory_space=pl.ANY)] * 2,
            out_specs=(vmem, vmem),
            scratch_shapes=[
                pltpu.VMEM(tensor.shape, F32),
                pltpu.VMEM(isometries.shape, F32),
                pltpu.VMEM((levels, parts, 2 * rows, width2 // 2), F32),
                pltpu.VMEM((parts, 1, 128), F32),
                pltpu.VMEM((1, 1, 128), F32),
                pltpu.VMEM((rows * width // 2, 128), F32),
                pltpu.VMEM((rows * width, 128), F32),
                pltpu.VMEM((width // 2, 2 * width, 128), BF16),
                pltpu.VMEM((width2 // 2, 128), F32),
                pltpu.VMEM((2, rows * width, 128), BF16),
                pltpu.VMEM((rows // 2, width2, 128), BF16),
                pltpu.VMEM((rows // 2, width2, 128), BF16),
                pltpu.VMEM((128, 128), F32),
                dma((levels, 2, 1 + 2 * PIECES + PIECES // 2)),
                dma((levels, 2)),
                dma((levels,)),
                dma((1,)),
                dma((1,)),
                dma((2,)),
            ],
            compiler_params=pltpu.CompilerParams(collective_id=0, has_side_effects=True),
        )(tensor, isometries)
        return out, log_density[0, :1]

    in_specs = (P(("temp", "bond"), None), P("temp", "bond", None))
    out_specs = (P(("temp", "bond"), None), P("temp"))
    return jax.shard_map(on_device, mesh=mesh, in_specs=in_specs, out_specs=out_specs, check_vma=False)
```
